32 devices in a mesh: ep: 8 (over z, x), tp: 4 (over y, core).
Axes of the slice: x: 2, y: 2, z: 4, core: 2. Of those that a mesh axis runs over, the one named last changes fastest.
Arguments:
- hidden_in: bfloat16 [1024, 2048], P('ep', 'tp'), may hold values from -6 to 6
- norm_gain: float32 [2048], replicated, may hold values from 0.5 to 1.5
- router_weight: bfloat16 [2048, 8], replicated, may hold values from -4.861359 to 4.861359
- shared_gate_up: bfloat16 [2048, 2, 1408], P(None, None, 'tp'), may hold values from -0.125 to 0.125
- shared_down: bfloat16 [1408, 2048], P('tp'), may hold values from -0.15625 to 0.15625
- slot_gate_up: bfloat16 [32, 2048, 2, 704], P(('ep', 'tp')), as said below
- slot_down: bfloat16 [32, 704, 2048], P(('ep', 'tp')), as said below
- slot_expert: int32 [32], replicated, may hold values from 0 to 7, as said below
- slot_choice: int32 [1024, 6], P('ep'), may hold values from 0 to 31, all different within a row; in each aligned block of 32 rows (0 to 31, 32 to 63, ...) at most 12 rows name the same one
- live_count: int32 [8], P('ep'), may hold values from 64 to 128, as said below
Outputs:
- mixed_out: bfloat16 [1024, 2048], P('ep', 'tp')
The draws below stay inside these ranges and needn't reach their ends.
Inputs may be any that keep to these rules, and one draw needn't show every extreme that they name: `slot_expert`: each expert is held by 1 or 7 slots; exactly 4 experts by the larger number. `slot_gate_up`: entry s holds the weights of expert slot_expert[s]; slots of one expert hold equal weights. `slot_down`: entry s holds the weights of expert slot_expert[s]; slots of one expert hold equal weights. `slot_choice`: a row names 6 different slots; in each aligned block of 32 rows no slot is named more than 12 times. `live_count`: the live rows of an index of ep are its first ones; some index of ep has all 128 rows live.
All inputs are finite; a program needn't handle non-finite values.
Results may differ from the reference program's by a relative error of at most 0.0058.
Values may be sent and summed in bfloat16 or wider, within the bound.
A program may use at most 64 MiB of HBM per device.

```python
import math
import jax
import jax.numpy as jnp
import numpy as np
from jax import lax

D = 2048
EXP_FF = 704
SHARED_FF = 1408
TOP = 6
TOK_DEV = 128
EXPERTS = 8
SLOTS = 32
CAP = 12
TOKENS = 1024
N_EP = 8
N_TP = 4


def placement_table(key):
    copies = 2 * (SLOTS // EXPERTS) - 1
    shuffled = jax.random.permutation(jax.random.fold_in(key, 11), EXPERTS).astype(jnp.int32)
    hot_half = shuffled[:EXPERTS // 2]
    listed = jnp.concatenate([jnp.tile(hot_half, copies), shuffled[EXPERTS // 2:]])
    mixing = jax.random.permutation(jax.random.fold_in(key, 12), SLOTS)
    return listed[mixing].astype(jnp.int32)


def expert_block(weight_key, expert, shape, fan_in):
    sub_key = jax.random.fold_in(weight_key, expert)
    values = jax.random.normal(sub_key, shape, jnp.float32)
    return (values * fan_in ** (-0.5)).astype(jnp.bfloat16)


def draw_slot_expert(key, part):
    return placement_table(key)


def draw_slot_gate_up(key, part):
    slot_table = placement_table(key)
    weight_key = jax.random.fold_in(key, 21)
    return lax.map(lambda expert: expert_block(weight_key, expert, (D, 2, EXP_FF), D), slot_table)


def draw_slot_down(key, part):
    slot_table = placement_table(key)
    weight_key = jax.random.fold_in(key, 22)
    return lax.map(lambda expert: expert_block(weight_key, expert, (EXP_FF, D), EXP_FF), slot_table)


def draw_router_weight(key, part):
    base = jax.random.normal(jax.random.fold_in(key, 31), (D, EXPERTS), jnp.float32)
    column_scale = jnp.exp(jax.random.uniform(jax.random.fold_in(key, 34), (EXPERTS,), jnp.float32, -1.2, 0.0))
    matrix = base * column_scale
    return (matrix * D ** (-0.5)).astype(jnp.bfloat16)


def draw_live_count(key, part):
    counts = jax.random.randint(jax.random.fold_in(key, 41), (N_EP,), TOK_DEV // 2, TOK_DEV + 1)
    fullest = jax.random.randint(jax.random.fold_in(key, 42), (), 0, N_EP)
    return jnp.where(jnp.arange(N_EP) == fullest, TOK_DEV, counts).astype(jnp.int32)


def levels(key, shape, cuts, smallest, top_value):
    loudness = 1.0
    for dim, blocks in cuts:
        draws = jax.random.uniform(jax.random.fold_in(jax.random.fold_in(key, 6), dim), (blocks,), jnp.float32, smallest / len(cuts), top_value / len(cuts))
        loudness = loudness * jnp.repeat(jnp.exp(draws), shape[dim] // blocks).reshape((-1,) + (1,) * (len(shape) - 1 - dim))
    return loudness


def assign_block(key, own, number, rows, amount, top, most, slope):
    ranking = jax.random.permutation(key, amount)
    crowded, usual = shares(amount, rows * top, most, slope, True), shares(amount, rows * top, most, slope, False)
    places = jnp.arange(amount)

    def named(tallies, offset_by):
        used = int((tallies > 0).sum())
        fixed = max(1, used // 4)
        passed = fixed + (places - fixed + offset_by * (used - fixed)) % max(1, amount - fixed)
        return jnp.zeros((amount,), jnp.int32).at[ranking[jnp.where(places < fixed, places, passed)]].set(jnp.asarray(tallies, jnp.int32))

    tallies = jnp.where(number % 4 == 0, named(crowded, number // 4), named(usual, number - number // 4 - 1))
    mixed = jax.random.permutation(jax.random.fold_in(own, 3), amount)
    source_of, receiver = mixed[0:amount // 2 * 2:2], mixed[1:amount // 2 * 2:2]
    margin = jnp.minimum(tallies[source_of] - 1, most - tallies[receiver]) // 2
    margin = jnp.where((source_of == ranking[0]) | (receiver == ranking[0]) | (tallies[receiver] == 0), 0, jnp.maximum(margin, 0))
    passed = jax.random.randint(jax.random.fold_in(own, 4), (amount // 2,), 0, 1 << 20) % (margin + 1)
    tallies = tallies.at[source_of].add(-passed).at[receiver].add(passed)
    items = jnp.searchsorted(jnp.cumsum(tallies), jnp.arange(rows * top), side="right").astype(jnp.int32)
    grid = items.reshape(top, rows).T
    grid = grid[jax.random.permutation(jax.random.fold_in(own, 1), rows)]
    offset_by = jax.random.randint(jax.random.fold_in(own, 2), (rows, 1), 0, top)
    return jnp.take_along_axis(grid, (jnp.arange(top)[None, :] + offset_by) % top, axis=1)


def shares(number_of, total, reach, slope, full):
    portions = [(1 << 20) // math.isqrt(rank ** slope) + 1 for rank in range(1, number_of + 1)]
    largest = reach if full else min(reach, max(-(-total // number_of), total * portions[0] // sum(portions)))
    least = 1 if total - largest >= number_of - 1 else 0
    given, surplus = [largest] + [least] * (number_of - 1), total - largest - least * (number_of - 1)
    while surplus > 0:
        free = [i for i in range(1, number_of) if given[i] < largest] or [i for i in range(1, number_of) if given[i] < reach]
        whole, remaining = sum([portions[i] for i in free]), surplus
        for i in free:
            more = min(reach - given[i], max(1, remaining * portions[i] // whole), surplus)
            given[i] = given[i] + more
            surplus = surplus - more
    return np.array(given)


def noise(stream_key, extent, deviation, bound, split=(), held_as=jnp.bfloat16):
    drawn = deviation * jax.random.normal(stream_key, extent, jnp.float32)
    if split:
        drawn = drawn * levels(stream_key, extent, split, -0.22, 0.18)
    return jnp.clip(drawn, -bound, bound).astype(held_as)


def setup_inputs(seed: int = 0) -> dict:
    streams_of = jax.random.split(jax.random.key(seed), 11)
    hidden_in = noise(streams_of[0], (TOKENS, D), 1.0, 6.0, ((0, 8), (1, 4)))
    norm_gain = jnp.clip(1.0 + 0.1 * jax.random.normal(streams_of[1], (D,), jnp.float32), 0.5, 1.5)
    router_weight = draw_router_weight(jax.random.fold_in(streams_of[10], 71), 0)
    shared_gate_up = noise(streams_of[3], (D, 2, SHARED_FF), D ** -0.5, 0.125, ((2, 4),))
    shared_down = noise(streams_of[4], (SHARED_FF, D), SHARED_FF ** -0.5, 0.15625, ((0, 4),))
    slot_gate_up = draw_slot_gate_up(jax.random.fold_in(streams_of[10], 71), 0)
    slot_down = draw_slot_down(jax.random.fold_in(streams_of[10], 71), 0)
    slot_expert = draw_slot_expert(jax.random.fold_in(streams_of[10], 71), 0)
    slot_choice_keys = jax.random.split(jax.random.fold_in(streams_of[8], 1), TOKENS // (TOK_DEV // N_TP))
    slot_choice_turns = jax.random.permutation(jax.random.fold_in(streams_of[8], 3), TOKENS // (TOK_DEV // N_TP))
    slot_choice = jax.vmap(lambda own, number: assign_block(jax.random.fold_in(streams_of[8], 2), own, number, TOK_DEV // N_TP, SLOTS, TOP, CAP, 2))(slot_choice_keys, slot_choice_turns).reshape((TOKENS, TOP))
    live_count = draw_live_count(jax.random.fold_in(streams_of[10], 71), 0)
    return dict(hidden_in=hidden_in, norm_gain=norm_gain, router_weight=router_weight, shared_gate_up=shared_gate_up, shared_down=shared_down, slot_gate_up=slot_gate_up, slot_down=slot_down, slot_expert=slot_expert, slot_choice=slot_choice, live_count=live_count)


def reference(hidden_in, norm_gain, router_weight, shared_gate_up, shared_down, slot_gate_up, slot_down, slot_expert, slot_choice, live_count):
    wide_rows = hidden_in.astype(jnp.float32)
    norm_scale = lax.rsqrt(lax.optimization_barrier(jnp.mean(wide_rows * wide_rows, axis=1, keepdims=True)) + 1e-06)
    normed = (wide_rows * norm_scale * norm_gain).astype(jnp.bfloat16)
    logits = jnp.dot(normed, router_weight, preferred_element_type=jnp.float32)
    expert_ids = slot_expert[slot_choice].astype(jnp.int32)
    picked = jnp.take_along_axis(logits, expert_ids, axis=1)
    gate_values = jax.nn.softmax(picked, axis=1).astype(jnp.bfloat16)
    shared_proj = jnp.einsum('td,dgf->tgf', normed.astype(jnp.float32), shared_gate_up.astype(jnp.float32))
    shared_hidden = (jax.nn.silu(shared_proj[:, 0]) * shared_proj[:, 1]).astype(jnp.bfloat16)
    shared_out = jnp.dot(shared_hidden.astype(jnp.float32), shared_down.astype(jnp.float32), preferred_element_type=jnp.float32)
    depth = TOKENS // (TOK_DEV // N_TP) * CAP
    flat_slots = slot_choice.reshape(-1).astype(jnp.int32)
    ordering = jnp.argsort(flat_slots, stable=True).astype(jnp.int32)
    sorted_slots = flat_slots[ordering]
    slot_range = jnp.arange(SLOTS, dtype=jnp.int32)
    firsts = jnp.searchsorted(sorted_slots, slot_range, side='left').astype(jnp.int32)
    lasts = jnp.searchsorted(sorted_slots, slot_range, side='right').astype(jnp.int32)
    padded_order = jnp.concatenate([ordering, jnp.zeros((depth,), jnp.int32)])
    flat_gates = gate_values.reshape(-1).astype(jnp.float32)

    def visit_slot(routed_sum, slot_index):
        pick_ids = lax.dynamic_slice_in_dim(padded_order, firsts[slot_index], depth)
        in_range = jnp.arange(depth, dtype=jnp.int32) < lasts[slot_index] - firsts[slot_index]
        token_ids = (pick_ids // TOP).astype(jnp.int32)
        inputs = normed[token_ids].astype(jnp.float32)
        gate_up = jnp.einsum('rd,dgf->rgf', inputs, slot_gate_up[slot_index].astype(jnp.float32))
        activated = (jax.nn.silu(gate_up[:, 0]) * gate_up[:, 1]).astype(jnp.bfloat16)
        result = jnp.dot(activated.astype(jnp.float32), slot_down[slot_index].astype(jnp.float32), preferred_element_type=jnp.float32).astype(jnp.bfloat16)
        weight = jnp.where(in_range, flat_gates[pick_ids], jnp.zeros_like(flat_gates[pick_ids]))
        routed_sum = routed_sum.at[token_ids].add(weight[:, None] * result.astype(jnp.float32))
        return (routed_sum, None)
    routed_pair = lax.scan(visit_slot, jnp.zeros((TOKENS, D), jnp.float32), slot_range)
    routed = routed_pair[0]
    positions = jnp.arange(TOKENS, dtype=jnp.int32)
    live_rows = positions % TOK_DEV < live_count[positions // TOK_DEV]
    mixed_out = jnp.where(live_rows[:, None], wide_rows + shared_out + routed, jnp.zeros_like(routed))
    return mixed_out.astype(jnp.bfloat16)
```

```python
import jax
import jax.numpy as jnp
from jax import lax
from jax.sharding import PartitionSpec as P


def gate_weights(normed_rows, choices, router_weight, slot_expert):
    logits = jnp.dot(normed_rows, router_weight, preferred_element_type=jnp.float32)
    slot_total = slot_expert.shape[0]
    expert_total = router_weight.shape[1]
    slot_hit = choices[:, :, None] == jnp.arange(slot_total, dtype=jnp.int32)
    expert_ids = jnp.sum(jnp.where(slot_hit, slot_expert, 0), axis=2)
    expert_hit = expert_ids[:, :, None] == jnp.arange(expert_total, dtype=jnp.int32)
    picked = jnp.sum(jnp.where(expert_hit, logits[:, None, :], 0.0), axis=2)
    highest = jnp.max(picked, axis=1, keepdims=True)
    weights = jnp.exp(picked - highest)
    return (weights / jnp.sum(weights, axis=1, keepdims=True)).astype(jnp.bfloat16)


def slot_positions(targets):
    length = targets.shape[0]
    same_slot = targets[:, None] == targets[None, :]
    earlier = jnp.arange(length)[None, :] < jnp.arange(length)[:, None]
    return jnp.sum(same_slot & earlier, axis=1)


def expert_apply(received, slot_gate_up, slot_down):
    shape_in = received.shape
    flat_rows = received.reshape(-1, shape_in[-1])
    gate_up = jnp.einsum(
        "rd,dgf->rgf", flat_rows, slot_gate_up[0], preferred_element_type=jnp.float32
    )
    activated = (jax.nn.silu(gate_up[:, 0]) * gate_up[:, 1]).astype(jnp.bfloat16)
    result = jnp.dot(activated, slot_down[0], preferred_element_type=jnp.float32).astype(
        jnp.bfloat16
    )
    return result.reshape(shape_in)


def local_exchange(
    hidden_in,
    norm_gain,
    router_weight,
    shared_gate_up,
    shared_down,
    slot_gate_up,
    slot_down,
    slot_expert,
    slot_choice,
    live_count,
):
    tp_count = lax.axis_size("tp")
    ep_count = lax.axis_size("ep")
    tp_index = lax.axis_index("tp")
    tok_count = hidden_in.shape[0]
    feature_width = hidden_in.shape[1] * tp_count
    top_count = slot_choice.shape[1]
    slot_count = slot_expert.shape[0]
    quarter = tok_count // tp_count
    capacity = max(2, 2 * quarter * top_count // slot_count)
    full_rows = lax.all_gather(hidden_in, "tp", axis=1, tiled=True)
    wide_rows = full_rows.astype(jnp.float32)
    norm_scale = lax.rsqrt(jnp.mean(wide_rows * wide_rows, axis=1, keepdims=True) + 1e-06)
    normed = (wide_rows * norm_scale * norm_gain).astype(jnp.bfloat16)
    shared_proj = jnp.einsum(
        "td,dgf->tgf", normed, shared_gate_up, preferred_element_type=jnp.float32
    )
    shared_hidden = (jax.nn.silu(shared_proj[:, 0]) * shared_proj[:, 1]).astype(jnp.bfloat16)
    partial_value = jnp.dot(shared_hidden, shared_down, preferred_element_type=jnp.float32)
    row_start = tp_index * quarter
    own_rows = lax.dynamic_slice_in_dim(normed, row_start, quarter, 0)
    own_choice = lax.dynamic_slice_in_dim(slot_choice, row_start, quarter, 0)
    gate_values = gate_weights(own_rows, own_choice, router_weight, slot_expert)
    targets = own_choice.reshape(-1)
    placed = targets * capacity + slot_positions(targets)
    outgoing = jnp.zeros((slot_count * capacity, feature_width), jnp.bfloat16)
    outgoing = outgoing.at[placed].set(jnp.repeat(own_rows, top_count, axis=0))
    outgoing = outgoing.reshape(ep_count, tp_count, capacity, feature_width)
    arrived = lax.all_to_all(
        lax.all_to_all(outgoing, "ep", split_axis=0, concat_axis=0, tiled=True),
        "tp",
        split_axis=1,
        concat_axis=1,
        tiled=True,
    )
    computed = expert_apply(arrived, slot_gate_up, slot_down)
    returned = lax.all_to_all(
        lax.all_to_all(computed, "ep", split_axis=0, concat_axis=0, tiled=True),
        "tp",
        split_axis=1,
        concat_axis=1,
        tiled=True,
    )
    fetched = returned.reshape(-1, feature_width)[placed].reshape(quarter, top_count, feature_width)
    routed = jnp.einsum("qk,qkd->qd", gate_values, fetched, preferred_element_type=jnp.float32)
    own_partial = lax.dynamic_slice_in_dim(partial_value, row_start, quarter, 0) + routed
    partial_value = lax.dynamic_update_slice_in_dim(partial_value, own_partial, row_start, 0)
    summed = lax.psum_scatter(partial_value, "tp", scatter_dimension=1, tiled=True)
    live_rows = jnp.arange(tok_count, dtype=jnp.int32) < live_count[0]
    mixed_out = jnp.where(live_rows[:, None], hidden_in.astype(jnp.float32) + summed, 0.0)
    return mixed_out.astype(jnp.bfloat16)


def local_dense(
    hidden_in,
    norm_gain,
    router_weight,
    shared_gate_up,
    shared_down,
    slot_gate_up,
    slot_down,
    slot_expert,
    slot_choice,
    live_count,
):
    tp_count = lax.axis_size("tp")
    ep_count = lax.axis_size("ep")
    ep_index = lax.axis_index("ep")
    me = ep_index * tp_count + lax.axis_index("tp")
    tok_count, part_width = hidden_in.shape
    feature_width = part_width * tp_count
    top_count = slot_choice.shape[1]
    slot_count = slot_expert.shape[0]
    quarter = tok_count // tp_count
    capacity = tp_count * max(2, 2 * quarter * top_count // slot_count)
    blocks = lax.all_gather(hidden_in, ("ep", "tp"), axis=0)
    choices = lax.all_gather(slot_choice, "ep", axis=0, tiled=True)
    blocks = blocks.reshape(ep_count, tp_count, tok_count, part_width)
    full_rows = blocks.transpose(0, 2, 1, 3).reshape(ep_count * tok_count, feature_width)
    wide_rows = full_rows.astype(jnp.float32)
    norm_scale = lax.rsqrt(jnp.mean(wide_rows * wide_rows, axis=1, keepdims=True) + 1e-06)
    normed = (wide_rows * norm_scale * norm_gain).astype(jnp.bfloat16)
    gate_values = gate_weights(normed, choices, router_weight, slot_expert)
    mine = choices == me
    hit = jnp.any(mine, axis=1).reshape(ep_count, tok_count)
    gate = jnp.sum(jnp.where(mine, gate_values, 0).astype(jnp.float32), axis=1)
    gate = gate.reshape(ep_count, tok_count)
    earlier = jnp.arange(tok_count)[:, None] < jnp.arange(tok_count)[None, :]
    place = jnp.dot(
        hit.astype(jnp.bfloat16), earlier.astype(jnp.bfloat16), preferred_element_type=jnp.float32
    ).astype(jnp.int32)
    chosen = hit[:, None, :] & (place[:, None, :] == jnp.arange(capacity)[None, :, None])
    blocked = normed.reshape(ep_count, tok_count, feature_width)
    picked = jnp.einsum(
        "bcr,brd->bcd",
        chosen.astype(jnp.bfloat16),
        blocked,
        preferred_element_type=jnp.float32,
    ).astype(jnp.bfloat16)
    computed = expert_apply(picked, slot_gate_up, slot_down)
    spread = jnp.where(chosen, gate[:, None, :], 0.0).astype(jnp.bfloat16)
    routed = jnp.einsum("bcr,bcd->brd", spread, computed, preferred_element_type=jnp.float32)
    own_rows = lax.dynamic_index_in_dim(blocked, ep_index, 0, keepdims=False)
    shared_proj = jnp.einsum(
        "td,dgf->tgf", own_rows, shared_gate_up, preferred_element_type=jnp.float32
    )
    shared_hidden = (jax.nn.silu(shared_proj[:, 0]) * shared_proj[:, 1]).astype(jnp.bfloat16)
    shared_part = jnp.dot(shared_hidden, shared_down, preferred_element_type=jnp.float32)
    own_block = jnp.arange(ep_count)[:, None, None] == ep_index
    partial = (routed + jnp.where(own_block, shared_part[None], 0.0)).astype(jnp.bfloat16)
    partial = partial.reshape(ep_count, tok_count, tp_count, part_width).transpose(0, 2, 1, 3)
    partial = partial.reshape(ep_count * tp_count, tok_count, part_width)
    summed = lax.psum_scatter(partial, ("ep", "tp"), scatter_dimension=0)
    live_rows = jnp.arange(tok_count, dtype=jnp.int32) < live_count[0]
    mixed_out = jnp.where(
        live_rows[:, None], hidden_in.astype(jnp.float32) + summed.astype(jnp.float32), 0.0
    )
    return mixed_out.astype(jnp.bfloat16)


def solution(mesh):
    in_specs = (
        P("ep", "tp"),
        P(),
        P(),
        P(None, None, "tp"),
        P("tp", None),
        P(("ep", "tp"), None, None, None),
        P(("ep", "tp"), None, None),
        P(),
        P("ep", None),
        P("ep"),
    )
    out_specs = P("ep", "tp")
    local = local_dense if mesh.size <= 64 else local_exchange
    return jax.shard_map(local, mesh=mesh, in_specs=in_specs, out_specs=out_specs, check_vma=False)
```

```python
import functools
import jax
import jax.numpy as jnp
from jax import lax
from jax.experimental import pallas as pl
from jax.experimental.pallas import tpu as pltpu
from jax.sharding import PartitionSpec as P


def gate_weights(normed_rows, choices, router_weight, slot_expert):
    logits = jnp.dot(normed_rows, router_weight, preferred_element_type=jnp.float32)
    slot_total = slot_expert.shape[0]
    expert_total = router_weight.shape[1]
    slot_hit = choices[:, :, None] == jnp.arange(slot_total, dtype=jnp.int32)
    expert_ids = jnp.sum(jnp.where(slot_hit, slot_expert, 0), axis=2)
    expert_hit = expert_ids[:, :, None] == jnp.arange(expert_total, dtype=jnp.int32)
    picked = jnp.sum(jnp.where(expert_hit, logits[:, None, :], 0.0), axis=2)
    highest = jnp.max(picked, axis=1, keepdims=True)
    weights = jnp.exp(picked - highest)
    return (weights / jnp.sum(weights, axis=1, keepdims=True)).astype(jnp.bfloat16)


def slot_positions(targets):
    length = targets.shape[0]
    same_slot = targets[:, None] == targets[None, :]
    earlier = jnp.arange(length)[None, :] < jnp.arange(length)[:, None]
    return jnp.sum(same_slot & earlier, axis=1)


def expert_apply(received, slot_gate_up, slot_down):
    shape_in = received.shape
    flat_rows = received.reshape(-1, shape_in[-1])
    gate_up = jnp.einsum(
        "rd,dgf->rgf", flat_rows, slot_gate_up[0], preferred_element_type=jnp.float32
    )
    activated = (jax.nn.silu(gate_up[:, 0]) * gate_up[:, 1]).astype(jnp.bfloat16)
    result = jnp.dot(activated, slot_down[0], preferred_element_type=jnp.float32).astype(
        jnp.bfloat16
    )
    return result.reshape(shape_in)


def local_exchange(
    hidden_in,
    norm_gain,
    router_weight,
    shared_gate_up,
    shared_down,
    slot_gate_up,
    slot_down,
    slot_expert,
    slot_choice,
    live_count,
):
    tp_count = lax.axis_size("tp")
    ep_count = lax.axis_size("ep")
    tp_index = lax.axis_index("tp")
    tok_count = hidden_in.shape[0]
    feature_width = hidden_in.shape[1] * tp_count
    top_count = slot_choice.shape[1]
    slot_count = slot_expert.shape[0]
    quarter = tok_count // tp_count
    capacity = max(2, 2 * quarter * top_count // slot_count)
    full_rows = lax.all_gather(hidden_in, "tp", axis=1, tiled=True)
    wide_rows = full_rows.astype(jnp.float32)
    norm_scale = lax.rsqrt(jnp.mean(wide_rows * wide_rows, axis=1, keepdims=True) + 1e-06)
    normed = (wide_rows * norm_scale * norm_gain).astype(jnp.bfloat16)
    shared_proj = jnp.einsum(
        "td,dgf->tgf", normed, shared_gate_up, preferred_element_type=jnp.float32
    )
    shared_hidden = (jax.nn.silu(shared_proj[:, 0]) * shared_proj[:, 1]).astype(jnp.bfloat16)
    partial_value = jnp.dot(shared_hidden, shared_down, preferred_element_type=jnp.float32)
    row_start = tp_index * quarter
    own_rows = lax.dynamic_slice_in_dim(normed, row_start, quarter, 0)
    own_choice = lax.dynamic_slice_in_dim(slot_choice, row_start, quarter, 0)
    gate_values = gate_weights(own_rows, own_choice, router_weight, slot_expert)
    targets = own_choice.reshape(-1)
    placed = targets * capacity + slot_positions(targets)
    outgoing = jnp.zeros((slot_count * capacity, feature_width), jnp.bfloat16)
    outgoing = outgoing.at[placed].set(jnp.repeat(own_rows, top_count, axis=0))
    outgoing = outgoing.reshape(ep_count, tp_count, capacity, feature_width)
    arrived = lax.all_to_all(
        lax.all_to_all(outgoing, "ep", split_axis=0, concat_axis=0, tiled=True),
        "tp",
        split_axis=1,
        concat_axis=1,
        tiled=True,
    )
    computed = expert_apply(arrived, slot_gate_up, slot_down)
    returned = lax.all_to_all(
        lax.all_to_all(computed, "ep", split_axis=0, concat_axis=0, tiled=True),
        "tp",
        split_axis=1,
        concat_axis=1,
        tiled=True,
    )
    fetched = returned.reshape(-1, feature_width)[placed].reshape(quarter, top_count, feature_width)
    routed = jnp.einsum("qk,qkd->qd", gate_values, fetched, preferred_element_type=jnp.float32)
    own_partial = lax.dynamic_slice_in_dim(partial_value, row_start, quarter, 0) + routed
    partial_value = lax.dynamic_update_slice_in_dim(partial_value, own_partial, row_start, 0)
    summed = lax.psum_scatter(partial_value, "tp", scatter_dimension=1, tiled=True)
    live_rows = jnp.arange(tok_count, dtype=jnp.int32) < live_count[0]
    mixed_out = jnp.where(live_rows[:, None], hidden_in.astype(jnp.float32) + summed, 0.0)
    return mixed_out.astype(jnp.bfloat16)


def dot_nt(a, b):
    return lax.dot_general(a, b, (((1,), (1,)), ((), ())), preferred_element_type=jnp.float32)


def dot_nn(a, b):
    return jnp.dot(a, b, preferred_element_type=jnp.float32)


def silu_mul(g, u):
    return (g / (1.0 + jnp.exp(-g)) * u).astype(jnp.bfloat16)


def chunks(total, step):
    return [(at, min(step, total - at)) for at in range(0, total, step)]


def block_kernel(
    nz,
    cap,
    top,
    hid,
    ch_own,
    slot_col,
    gain,
    router_t,
    w_gu,
    w_d,
    w_sgu,
    w_sd,
    out,
    xbuf,
    cbuf,
    gu,
    dn,
    sgu,
    sdn,
    hits,
    member,
    cho,
    chg,
    raw,
    sel,
    hmid,
    expo,
    own,
    hsh,
    shp,
    keep,
    snd,
    crecv,
    dsum,
    ry0,
    rx1,
    xs,
    ys,
    rxf,
    ryf,
    osum,
    rz,
    wsem,
    ssem,
    rsem,
):
    bf16, f32 = jnp.bfloat16, jnp.float32
    ep, tp = lax.axis_index("ep"), lax.axis_index("tp")
    z, x, y, c = ep // 2, ep % 2, tp // 2, tp % 2
    tok, width = hid.shape
    half = tok // 2
    feat = gain.shape[1]
    slots = slot_col.shape[0]
    me = ep * 4 + tp

    def at_ep(j, i):
        return lax.rem(z + j, nz) * 2 + (1 - x if i else x)

    def at_tp(k, l):
        return (1 - y if k else y) * 2 + (1 - c if l else c)

    def cols(k, l):
        return pl.ds(pl.multiple_of(at_tp(k, l) * width, width), width)

    x_dev, y_dev, c_dev = (at_ep(0, 1), tp), (ep, at_tp(1, 0)), (ep, at_tp(0, 1))
    peers = [(j, i) for j in range(nz) for i in range(2) if j or i]

    barrier = pltpu.get_barrier_semaphore()
    for j, i in peers:
        pl.semaphore_signal(
            barrier, inc=1, device_id=(at_ep(j, i), tp), device_id_type=pl.DeviceIdType.MESH
        )
    for dev in (y_dev, c_dev):
        pl.semaphore_signal(barrier, inc=1, device_id=dev, device_id_type=pl.DeviceIdType.MESH)
    loads = [
        pltpu.make_async_copy(src, dst, wsem.at[n])
        for n, (src, dst) in enumerate(((w_sgu, sgu), (w_sd, sdn), (w_gu, gu), (w_d, dn)))
    ]
    for load in loads:
        load.start()
    pl.semaphore_wait(barrier, len(peers) + 2)

    copies = {}

    def send(name, src, dst, dev):
        n = len(copies)
        copy = pltpu.make_async_remote_copy(
            src_ref=src,
            dst_ref=dst,
            send_sem=ssem.at[n],
            recv_sem=rsem.at[n],
            device_id=dev,
            device_id_type=pl.DeviceIdType.MESH,
        )
        copy.start()
        copies[name] = copy

    def got(*name):
        copies[name].wait_recv()

    back = lambda j: (nz - j) % nz
    lo, hi = pl.ds(0, half), pl.ds(half, half)

    for j in range(1, nz):
        send(("z", back(j)), hid, xbuf.at[back(j), 0, 0, 0], (at_ep(j, 0), tp))
    for j, i in peers:
        send(("ch", back(j), i), ch_own, cbuf.at[back(j) * 2 + i], (at_ep(j, i), tp))

    def spread(j):
        if j:
            got("z", j)
        src = xbuf.at[j, 0, 0, 0] if j else hid
        send(("x1", j), src, xbuf.at[j, 1, 0, 0], x_dev)
        send(("y1", j), src, xbuf.at[j, 0, 1, 0], y_dev)
        send(("c00", j), src, xbuf.at[j, 0, 0, 1], c_dev)

    def forward(j):
        got("x1", j)
        send(("y2", j), xbuf.at[j, 1, 0, 0, lo], xbuf.at[j, 1, 1, 0, lo], y_dev)
        send(("c10", j), xbuf.at[j, 1, 0, 0], xbuf.at[j, 1, 0, 1], c_dev)
        got("y1", j)
        send(("x2", j), xbuf.at[j, 0, 1, 0, hi], xbuf.at[j, 1, 1, 0, hi], x_dev)
        send(("c01", j), xbuf.at[j, 0, 1, 0], xbuf.at[j, 0, 1, 1], c_dev)

    def finish(j):
        got("y2", j)
        got("x2", j)
        send(("c11", j), xbuf.at[j, 1, 1, 0], xbuf.at[j, 1, 1, 1], c_dev)

    def select():
        cbuf[0] = ch_own[...]
        for j, i in peers:
            got("ch", j, i)
        slot_ids = lax.broadcasted_iota(jnp.int32, (slots, tok), 0)
        place = lax.broadcasted_iota(jnp.int32, (cap, tok), 0).astype(f32)
        members = []
        for q in range(2 * nz):
            picks = cbuf[q]
            named = jnp.zeros((slots, tok), f32)
            for k in range(top):
                named = jnp.where(picks[k : k + 1, :] == slot_ids, 1.0, named)
            hits[q : q + 1, :] = jnp.sum(
                jnp.where(slot_ids == me, named, 0.0), axis=0, keepdims=True
            )
            members.append(named.astype(bf16))
        earlier = lax.broadcasted_iota(jnp.int32, (tok, tok), 0) < lax.broadcasted_iota(
            jnp.int32, (tok, tok), 1
        )
        hit = hits[...]
        pos = dot_nn(hit.astype(bf16), jnp.where(earlier, 1.0, 0.0).astype(bf16))
        for q in range(2 * nz):
            chosen = jnp.where(place == pos[q : q + 1, :], hit[q : q + 1, :], 0.0).astype(bf16)
            cho[q] = chosen
            member[q * cap : (q + 1) * cap, :] = dot_nt(chosen, members[q])

    def norm(v):
        scale = lax.rsqrt(jnp.sum(v * v, axis=1, keepdims=True) * (1.0 / feat) + 1e-06)
        return (v * scale * gain[...]).astype(bf16)

    def pick(j, i):
        q = j * 2 + i
        for k in range(2):
            for l in range(2):
                raw[:, cols(k, l)] = dot_nn(cho[q], xbuf[j, i, k, l])
        sel[q * cap : (q + 1) * cap, :] = norm(raw[...])

    def shared():
        for k in range(2):
            for l in range(2):
                shp[:, cols(k, l)] = xbuf[0, 0, k, l].astype(f32)
        own[...] = norm(shp[...])
        loads[0].wait()
        ff = hsh.shape[1]
        hsh[...] = silu_mul(dot_nt(own[...], sgu[0:ff, :]), dot_nt(own[...], sgu[ff : 2 * ff, :]))
        loads[1].wait()
        for at, size in chunks(feat, 512):
            shp[:, at : at + size] = dot_nn(hsh[...], sdn[:, at : at + size])

    def experts():
        lanes = lax.broadcasted_iota(jnp.int32, (slots, router_t.shape[0]), 1)
        table = jnp.where(slot_col[...] == lanes, 1.0, 0.0).astype(bf16)
        by_slot = dot_nn(table, router_t[...]).astype(bf16)
        logits = dot_nt(sel[...], by_slot)
        named = member[...] > 0.5
        top_logit = jnp.max(jnp.where(named, logits, -1e30), axis=1, keepdims=True)
        weights = jnp.where(named, jnp.exp(jnp.where(named, logits - top_logit, 0.0)), 0.0)
        total = jnp.maximum(jnp.sum(weights, axis=1, keepdims=True), 1.0)
        slot_lane = lax.broadcasted_iota(jnp.int32, weights.shape, 1)
        mine = jnp.sum(jnp.where(slot_lane == me, weights, 0.0), axis=1, keepdims=True)
        gates = (mine / total).astype(bf16).astype(f32)
        for q in range(2 * nz):
            chg[q] = (cho[q].astype(f32) * gates[q * cap : (q + 1) * cap, :]).astype(bf16)
        loads[2].wait()
        ff = hmid.shape[1]
        for at, size in chunks(ff, 256):
            hmid[:, at : at + size] = silu_mul(
                dot_nt(sel[...], gu[at : at + size, :]),
                dot_nt(sel[...], gu[ff + at : ff + at + size, :]),
            )
        loads[3].wait()
        for at, size in chunks(feat, 512):
            expo[:, at : at + size] = dot_nn(hmid[...], dn[:, at : at + size]).astype(bf16)

    cbuf_ready = select
    xbuf[0, 0, 0, 0] = hid[...]
    spread(0)
    forward(0)
    for j in range(1, nz):
        spread(j)
        if j == 1:
            cbuf_ready()
        forward(j)
        finish(j - 1)
        for name in ("c00", "c10", "c01", "c11"):
            got(name, j - 1)
        if j == 1:
            shared()
        pick(j - 1, 0)
        pick(j - 1, 1)
    finish(nz - 1)
    for name in ("c00", "c10", "c01", "c11"):
        got(name, nz - 1)
    pick(nz - 1, 0)
    pick(nz - 1, 1)
    experts()

    def add(*refs):
        total = refs[0][...].astype(f32)
        for ref in refs[1:]:
            total = total + ref[...].astype(f32)
        return total

    def scatter(j):
        for i in (1, 0):
            q = j * 2 + i
            for l in (1, 0):
                for k in (1, 0):
                    part = lax.dot_general(
                        chg[q],
                        expo[q * cap : (q + 1) * cap, cols(k, l)],
                        (((0,), (0,)), ((), ())),
                        preferred_element_type=f32,
                    )
                    if q == 0:
                        part = part + shp[:, cols(k, l)]
                    (snd if l else keep)[j, i, k] = part.astype(bf16)
                if l:
                    send(("rc", j, i), snd.at[j, i], crecv.at[j, i], c_dev)

    def diagonal(j):
        got("rc", j, 1)
        dsum[j] = add(keep.at[j, 1, 1], crecv.at[j, 1, 1]).astype(bf16)
        send(("d0", j), dsum.at[j, lo], ry0.at[j], y_dev)
        send(("d1", j), dsum.at[j, hi], rx1.at[j], x_dev)

    def sides(j):
        xs[j, hi] = add(keep.at[j, 1, 0, hi], crecv.at[j, 1, 0, hi]).astype(bf16)
        got("d0", j)
        xs[j, lo] = add(keep.at[j, 1, 0, lo], crecv.at[j, 1, 0, lo], ry0.at[j]).astype(bf16)
        send(("rx", j), xs.at[j], rxf.at[j], x_dev)
        got("rc", j, 0)
        ys[j, lo] = add(keep.at[j, 0, 1, lo], crecv.at[j, 0, 1, lo]).astype(bf16)
        got("d1", j)
        ys[j, hi] = add(keep.at[j, 0, 1, hi], crecv.at[j, 0, 1, hi], rx1.at[j]).astype(bf16)
        send(("ry", j), ys.at[j], ryf.at[j], y_dev)

    def gather_sum(j):
        got("rx", j)
        got("ry", j)
        total = add(keep.at[j, 0, 0], crecv.at[j, 0, 0], rxf.at[j], ryf.at[j])
        if j:
            osum[j] = total.astype(bf16)
            send(("rz", j), osum.at[j], rz.at[j], (at_ep(j, 0), tp))
        else:
            out[...] = total

    order = sorted(range(1, nz), key=lambda j: -min(j, nz - j)) + [0]
    for t in range(nz + 3):
        for lag, stage in ((0, scatter), (1, diagonal), (2, sides), (3, gather_sum)):
            if 0 <= t - lag < nz:
                stage(order[t - lag])
    for j in range(1, nz):
        got("rz", j)
        out[...] += rz[j].astype(f32)
    for copy in copies.values():
        copy.wait_send()


def local_dense(
    hidden_in,
    norm_gain,
    router_weight,
    shared_gate_up,
    shared_down,
    slot_gate_up,
    slot_down,
    slot_expert,
    slot_choice,
    live_count,
):
    nz = lax.axis_size("ep") // 2
    tok_count, width = hidden_in.shape
    feat = 4 * width
    top_count = slot_choice.shape[1]
    slot_count = slot_expert.shape[0]
    cap = 4 * max(2, 2 * (tok_count // 4) * top_count // slot_count)
    rows = 2 * nz * cap
    sff, eff = shared_down.shape[0], slot_down.shape[1]
    choice_t = jnp.pad(slot_choice.T, ((0, 8 - top_count), (0, 0)), constant_values=-1)
    bf16, f32 = jnp.bfloat16, jnp.float32
    half = tok_count // 2
    block = (tok_count, width)
    vmem = pl.BlockSpec(memory_space=pltpu.VMEM)
    hbm = pl.BlockSpec(memory_space=pl.ANY)
    copy_count = (nz - 1) + (2 * nz - 1) + 3 * nz + 4 * nz + nz + 2 * nz + 4 * nz + (nz - 1)
    summed = pl.pallas_call(
        functools.partial(block_kernel, nz, cap, top_count),
        out_shape=jax.ShapeDtypeStruct(block, f32),
        in_specs=[vmem] * 5 + [hbm] * 4,
        out_specs=vmem,
        scratch_shapes=[
            pltpu.VMEM((nz, 2, 2, 2) + block, bf16),
            pltpu.VMEM((2 * nz, 8, tok_count), jnp.int32),
            pltpu.VMEM((2 * eff, feat), bf16),
            pltpu.VMEM((eff, feat), bf16),
            pltpu.VMEM((2 * sff, feat), bf16),
            pltpu.VMEM((sff, feat), bf16),
            pltpu.VMEM((2 * nz, tok_count), f32),
            pltpu.VMEM((rows, slot_count), f32),
            pltpu.VMEM((2 * nz, cap, tok_count), bf16),
            pltpu.VMEM((2 * nz, cap, tok_count), bf16),
            pltpu.VMEM((cap, feat), f32),
            pltpu.VMEM((rows, feat), bf16),
            pltpu.VMEM((rows, eff), bf16),
            pltpu.VMEM((rows, feat), bf16),
            pltpu.VMEM((tok_count, feat), bf16),
            pltpu.VMEM((tok_count, sff), bf16),
            pltpu.VMEM((tok_count, feat), f32),
            pltpu.VMEM((nz, 2, 2) + block, bf16),
            pltpu.VMEM((nz, 2, 2) + block, bf16),
            pltpu.VMEM((nz, 2, 2) + block, bf16),
            pltpu.VMEM((nz,) + block, bf16),
            pltpu.VMEM((nz, half, width), bf16),
            pltpu.VMEM((nz, half, width), bf16),
            pltpu.VMEM((nz,) + block, bf16),
            pltpu.VMEM((nz,) + block, bf16),
            pltpu.VMEM((nz,) + block, bf16),
            pltpu.VMEM((nz,) + block, bf16),
            pltpu.VMEM((nz,) + block, bf16),
            pltpu.VMEM((nz,) + block, bf16),
            pltpu.SemaphoreType.DMA((4,)),
            pltpu.SemaphoreType.DMA((copy_count,)),
            pltpu.SemaphoreType.DMA((copy_count,)),
        ],
        compiler_params=pltpu.CompilerParams(
            collective_id=0, has_side_effects=True, vmem_limit_bytes=56 * 2**20
        ),
    )(
        hidden_in,
        choice_t,
        slot_expert.reshape(-1, 1),
        norm_gain.reshape(1, -1),
        router_weight.T,
        slot_gate_up[0].transpose(1, 2, 0).reshape(2 * eff, feat),
        slot_down[0],
        shared_gate_up.transpose(1, 2, 0).reshape(2 * sff, feat),
        shared_down,
    )
    live_rows = jnp.arange(tok_count, dtype=jnp.int32) < live_count[0]
    mixed_out = jnp.where(live_rows[:, None], hidden_in.astype(jnp.float32) + summed, 0.0)
    return mixed_out.astype(jnp.bfloat16)


def solution(mesh):
    in_specs = (
        P("ep", "tp"),
        P(),
        P(),
        P(None, None, "tp"),
        P("tp", None),
        P(("ep", "tp"), None, None, None),
        P(("ep", "tp"), None, None),
        P(),
        P("ep", None),
        P("ep"),
    )
    out_specs = P("ep", "tp")
    local = local_dense if mesh.size <= 64 and mesh.shape["tp"] == 4 else local_exchange
    return jax.shard_map(local, mesh=mesh, in_specs=in_specs, out_specs=out_specs, check_vma=False)
```

```python
import functools
import jax
import jax.numpy as jnp
from jax import lax
from jax.experimental import pallas as pl
from jax.experimental.pallas import tpu as pltpu
from jax.sharding import PartitionSpec as P


def gate_weights(normed_rows, choices, router_weight, slot_expert):
    logits = jnp.dot(normed_rows, router_weight, preferred_element_type=jnp.float32)
    slot_total = slot_expert.shape[0]
    expert_total = router_weight.shape[1]
    slot_hit = choices[:, :, None] == jnp.arange(slot_total, dtype=jnp.int32)
    expert_ids = jnp.sum(jnp.where(slot_hit, slot_expert, 0), axis=2)
    expert_hit = expert_ids[:, :, None] == jnp.arange(expert_total, dtype=jnp.int32)
    picked = jnp.sum(jnp.where(expert_hit, logits[:, None, :], 0.0), axis=2)
    highest = jnp.max(picked, axis=1, keepdims=True)
    weights = jnp.exp(picked - highest)
    return (weights / jnp.sum(weights, axis=1, keepdims=True)).astype(jnp.bfloat16)


def slot_positions(targets):
    length = targets.shape[0]
    same_slot = targets[:, None] == targets[None, :]
    earlier = jnp.arange(length)[None, :] < jnp.arange(length)[:, None]
    return jnp.sum(same_slot & earlier, axis=1)


def expert_apply(received, slot_gate_up, slot_down):
    shape_in = received.shape
    flat_rows = received.reshape(-1, shape_in[-1])
    gate_up = jnp.einsum(
        "rd,dgf->rgf", flat_rows, slot_gate_up[0], preferred_element_type=jnp.float32
    )
    activated = (jax.nn.silu(gate_up[:, 0]) * gate_up[:, 1]).astype(jnp.bfloat16)
    result = jnp.dot(activated, slot_down[0], preferred_element_type=jnp.float32).astype(
        jnp.bfloat16
    )
    return result.reshape(shape_in)


def local_exchange(
    hidden_in,
    norm_gain,
    router_weight,
    shared_gate_up,
    shared_down,
    slot_gate_up,
    slot_down,
    slot_expert,
    slot_choice,
    live_count,
):
    tp_count = lax.axis_size("tp")
    ep_count = lax.axis_size("ep")
    tp_index = lax.axis_index("tp")
    tok_count = hidden_in.shape[0]
    feature_width = hidden_in.shape[1] * tp_count
    top_count = slot_choice.shape[1]
    slot_count = slot_expert.shape[0]
    quarter = tok_count // tp_count
    capacity = max(2, 2 * quarter * top_count // slot_count)
    full_rows = lax.all_gather(hidden_in, "tp", axis=1, tiled=True)
    wide_rows = full_rows.astype(jnp.float32)
    norm_scale = lax.rsqrt(jnp.mean(wide_rows * wide_rows, axis=1, keepdims=True) + 1e-06)
    normed = (wide_rows * norm_scale * norm_gain).astype(jnp.bfloat16)
    shared_proj = jnp.einsum(
        "td,dgf->tgf", normed, shared_gate_up, preferred_element_type=jnp.float32
    )
    shared_hidden = (jax.nn.silu(shared_proj[:, 0]) * shared_proj[:, 1]).astype(jnp.bfloat16)
    partial_value = jnp.dot(shared_hidden, shared_down, preferred_element_type=jnp.float32)
    row_start = tp_index * quarter
    own_rows = lax.dynamic_slice_in_dim(normed, row_start, quarter, 0)
    own_choice = lax.dynamic_slice_in_dim(slot_choice, row_start, quarter, 0)
    gate_values = gate_weights(own_rows, own_choice, router_weight, slot_expert)
    targets = own_choice.reshape(-1)
    placed = targets * capacity + slot_positions(targets)
    outgoing = jnp.zeros((slot_count * capacity, feature_width), jnp.bfloat16)
    outgoing = outgoing.at[placed].set(jnp.repeat(own_rows, top_count, axis=0))
    outgoing = outgoing.reshape(ep_count, tp_count, capacity, feature_width)
    arrived = lax.all_to_all(
        lax.all_to_all(outgoing, "ep", split_axis=0, concat_axis=0, tiled=True),
        "tp",
        split_axis=1,
        concat_axis=1,
        tiled=True,
    )
    computed = expert_apply(arrived, slot_gate_up, slot_down)
    returned = lax.all_to_all(
        lax.all_to_all(computed, "ep", split_axis=0, concat_axis=0, tiled=True),
        "tp",
        split_axis=1,
        concat_axis=1,
        tiled=True,
    )
    fetched = returned.reshape(-1, feature_width)[placed].reshape(quarter, top_count, feature_width)
    routed = jnp.einsum("qk,qkd->qd", gate_values, fetched, preferred_element_type=jnp.float32)
    own_partial = lax.dynamic_slice_in_dim(partial_value, row_start, quarter, 0) + routed
    partial_value = lax.dynamic_update_slice_in_dim(partial_value, own_partial, row_start, 0)
    summed = lax.psum_scatter(partial_value, "tp", scatter_dimension=1, tiled=True)
    live_rows = jnp.arange(tok_count, dtype=jnp.int32) < live_count[0]
    mixed_out = jnp.where(live_rows[:, None], hidden_in.astype(jnp.float32) + summed, 0.0)
    return mixed_out.astype(jnp.bfloat16)


def dot_nt(a, b):
    return lax.dot_general(a, b, (((1,), (1,)), ((), ())), preferred_element_type=jnp.float32)


def dot_nn(a, b):
    return jnp.dot(a, b, preferred_element_type=jnp.float32)


def silu_mul(g, u):
    return (g / (1.0 + jnp.exp(-g)) * u).astype(jnp.bfloat16)


def chunks(total, step):
    return [(at, min(step, total - at)) for at in range(0, total, step)]


def block_kernel(
    nz,
    cap,
    top,
    hid,
    ch_own,
    slot_row,
    gain,
    router_t,
    w_gu,
    w_d,
    w_sgu,
    w_sd,
    out,
    xbuf,
    cbuf,
    gu,
    dn,
    sgu,
    sdn,
    hits,
    by_slot,
    member,
    cho,
    chg,
    raw,
    sel,
    hmid,
    expo,
    own,
    hsh,
    shp,
    keep,
    snd,
    crecv,
    dsum,
    ry0,
    rx1,
    xs,
    ys,
    rxf,
    ryf,
    osum,
    rz,
    wsem,
    ssem,
    rsem,
):
    bf16, f32 = jnp.bfloat16, jnp.float32
    ep, tp = lax.axis_index("ep"), lax.axis_index("tp")
    z, x, y, c = ep // 2, ep % 2, tp // 2, tp % 2
    tok, width = hid.shape
    half = tok // 2
    feat = gain.shape[1]
    slots = slot_row.shape[1]
    me = ep * 4 + tp

    def at_ep(j, i):
        return lax.rem(z + j, nz) * 2 + (1 - x if i else x)

    def at_tp(k, l):
        return (1 - y if k else y) * 2 + (1 - c if l else c)

    def cols(k, l):
        return pl.ds(pl.multiple_of(at_tp(k, l) * width, width), width)

    x_dev, y_dev, c_dev = (at_ep(0, 1), tp), (ep, at_tp(1, 0)), (ep, at_tp(0, 1))
    peers = [(j, i) for j in range(nz) for i in range(2) if j or i]

    barrier = pltpu.get_barrier_semaphore()
    for j, i in peers:
        pl.semaphore_signal(
            barrier, inc=1, device_id=(at_ep(j, i), tp), device_id_type=pl.DeviceIdType.MESH
        )
    for dev in (y_dev, c_dev):
        pl.semaphore_signal(barrier, inc=1, device_id=dev, device_id_type=pl.DeviceIdType.MESH)
    loads = [
        pltpu.make_async_copy(src, dst, wsem.at[n])
        for n, (src, dst) in enumerate(((w_sgu, sgu), (w_sd, sdn), (w_gu, gu), (w_d, dn)))
    ]
    pl.semaphore_wait(barrier, len(peers) + 2)

    copies = {}

    def send(name, src, dst, dev):
        n = len(copies)
        copy = pltpu.make_async_remote_copy(
            src_ref=src,
            dst_ref=dst,
            send_sem=ssem.at[n],
            recv_sem=rsem.at[n],
            device_id=dev,
            device_id_type=pl.DeviceIdType.MESH,
        )
        copy.start()
        copies[name] = copy

    def got(*name):
        copies[name].wait_recv()

    back = lambda j: (nz - j) % nz
    lo, hi = pl.ds(0, half), pl.ds(half, half)

    order = sorted(range(nz), key=lambda j: min(j, nz - j))
    pos = {j: n for n, j in enumerate(order)}

    def send_rows():
        for j in order[1:]:
            send(("z", j), hid, xbuf.at[j, 0, 0, 0], (at_ep(back(j), 0), tp))

    def send_choices():
        for j, i in peers:
            send(("ch", j, i), ch_own, cbuf.at[pos[j] * 2 + i], (at_ep(back(j), i), tp))

    def spread(j):
        if j:
            got("z", j)
        src = xbuf.at[j, 0, 0, 0] if j else hid
        send(("x1", j), src, xbuf.at[j, 1, 0, 0], x_dev)
        send(("y1", j), src, xbuf.at[j, 0, 1, 0], y_dev)
        send(("c00", j), src, xbuf.at[j, 0, 0, 1], c_dev)

    def forward(j):
        got("x1", j)
        send(("y2", j), xbuf.at[j, 1, 0, 0, lo], xbuf.at[j, 1, 1, 0, lo], y_dev)
        send(("c10", j), xbuf.at[j, 1, 0, 0], xbuf.at[j, 1, 0, 1], c_dev)
        got("y1", j)
        send(("x2", j), xbuf.at[j, 0, 1, 0, hi], xbuf.at[j, 1, 1, 0, hi], x_dev)
        send(("c01", j), xbuf.at[j, 0, 1, 0], xbuf.at[j, 0, 1, 1], c_dev)

    def finish(j):
        got("y2", j)
        got("x2", j)
        send(("c11", j), xbuf.at[j, 1, 1, 0], xbuf.at[j, 1, 1, 1], c_dev)

    def select():
        cbuf[0] = ch_own[...]
        for j, i in peers:
            got("ch", j, i)
        slot_ids = lax.broadcasted_iota(jnp.int32, (slots, tok), 0)
        place = lax.broadcasted_iota(jnp.int32, (cap, tok), 0).astype(f32)
        members = []
        for q in range(2 * nz):
            picks = cbuf[q]
            named = jnp.zeros((slots, tok), f32)
            for k in range(top):
                named = jnp.where(picks[k : k + 1, :] == slot_ids, 1.0, named)
            hits[q : q + 1, :] = jnp.sum(
                jnp.where(slot_ids == me, named, 0.0), axis=0, keepdims=True
            )
            members.append(named.astype(bf16))
        earlier = lax.broadcasted_iota(jnp.int32, (tok, tok), 0) < lax.broadcasted_iota(
            jnp.int32, (tok, tok), 1
        )
        hit = hits[...]
        rank = dot_nn(hit.astype(bf16), jnp.where(earlier, 1.0, 0.0).astype(bf16))
        for q in range(2 * nz):
            chosen = jnp.where(place == rank[q : q + 1, :], hit[q : q + 1, :], 0.0).astype(bf16)
            cho[q] = chosen
            member[q * cap : (q + 1) * cap, :] = dot_nt(chosen, members[q])
        held = lax.broadcasted_iota(jnp.int32, (router_t.shape[0], slots), 0)
        table = jnp.where(slot_row[...] == held, 1.0, 0.0).astype(bf16)
        by_slot[...] = lax.dot_general(
            table, router_t[...], (((0,), (0,)), ((), ())), preferred_element_type=f32
        ).astype(bf16)

    def norm(v):
        scale = lax.rsqrt(jnp.sum(v * v, axis=1, keepdims=True) * (1.0 / feat) + 1e-06)
        return (v * scale * gain[...]).astype(bf16)

    def pick(j, i):
        q = pos[j] * 2 + i
        for k in range(2):
            for l in range(2):
                raw[:, cols(k, l)] = dot_nn(cho[q], xbuf[j, i, k, l])
        sel[q * cap : (q + 1) * cap, :] = norm(raw[...])

    def shared():
        for k in range(2):
            for l in range(2):
                shp[:, cols(k, l)] = xbuf[0, 0, k, l].astype(f32)
        own[...] = norm(shp[...])
        loads[0].wait()
        ff = hsh.shape[1]
        hsh[...] = silu_mul(dot_nt(own[...], sgu[0:ff, :]), dot_nt(own[...], sgu[ff : 2 * ff, :]))
        loads[1].wait()
        for at, size in chunks(feat, 512):
            shp[:, at : at + size] = dot_nn(hsh[...], sdn[:, at : at + size])

    def experts(js):
        first, last = 2 * min(pos[j] for j in js), 2 * max(pos[j] for j in js) + 2
        part = slice(first * cap, last * cap)
        logits = dot_nt(sel[part, :], by_slot[...])
        named = member[part, :] > 0.5
        top_logit = jnp.max(jnp.where(named, logits, -1e30), axis=1, keepdims=True)
        weights = jnp.where(named, jnp.exp(jnp.where(named, logits - top_logit, 0.0)), 0.0)
        total = jnp.maximum(jnp.sum(weights, axis=1, keepdims=True), 1.0)
        slot_lane = lax.broadcasted_iota(jnp.int32, weights.shape, 1)
        mine = jnp.sum(jnp.where(slot_lane == me, weights, 0.0), axis=1, keepdims=True)
        gates = (mine / total).astype(bf16).astype(f32)
        for q in range(first, last):
            at = (q - first) * cap
            chg[q] = (cho[q].astype(f32) * gates[at : at + cap, :]).astype(bf16)
        if first == 0:
            loads[2].wait()
        ff = hmid.shape[1]
        for at, size in chunks(ff, 256):
            hmid[part, at : at + size] = silu_mul(
                dot_nt(sel[part, :], gu[at : at + size, :]),
                dot_nt(sel[part, :], gu[ff + at : ff + at + size, :]),
            )
        if first == 0:
            loads[3].wait()
        for at, size in chunks(feat, 512):
            expo[part, at : at + size] = dot_nn(hmid[part, :], dn[:, at : at + size]).astype(bf16)

    def take(j):
        for name in ("c00", "c10", "c01", "c11"):
            got(name, j)
        if j == 0:
            shared()
        pick(j, 0)
        pick(j, 1)

    def add(*refs):
        total = refs[0][...].astype(f32)
        for ref in refs[1:]:
            total = total + ref[...].astype(f32)
        return total

    def scatter(j):
        for i in (1, 0):
            q = pos[j] * 2 + i
            for l in (1, 0):
                for k in (1, 0):
                    part = lax.dot_general(
                        chg[q],
                        expo[q * cap : (q + 1) * cap, cols(k, l)],
                        (((0,), (0,)), ((), ())),
                        preferred_element_type=f32,
                    )
                    if q == 0:
                        part = part + shp[:, cols(k, l)]
                    (snd if l else keep)[j, i, k] = part.astype(bf16)
                if l:
                    send(("rc", j, i), snd.at[j, i], crecv.at[j, i], c_dev)

    def diagonal(j):
        got("rc", j, 1)
        dsum[j] = add(keep.at[j, 1, 1], crecv.at[j, 1, 1]).astype(bf16)
        send(("d0", j), dsum.at[j, lo], ry0.at[j], y_dev)
        send(("d1", j), dsum.at[j, hi], rx1.at[j], x_dev)

    def sides(j):
        xs[j, hi] = add(keep.at[j, 1, 0, hi], crecv.at[j, 1, 0, hi]).astype(bf16)
        got("d0", j)
        xs[j, lo] = add(keep.at[j, 1, 0, lo], crecv.at[j, 1, 0, lo], ry0.at[j]).astype(bf16)
        send(("rx", j), xs.at[j], rxf.at[j], x_dev)
        got("rc", j, 0)
        ys[j, lo] = add(keep.at[j, 0, 1, lo], crecv.at[j, 0, 1, lo]).astype(bf16)
        got("d1", j)
        ys[j, hi] = add(keep.at[j, 0, 1, hi], crecv.at[j, 0, 1, hi], rx1.at[j]).astype(bf16)
        send(("ry", j), ys.at[j], ryf.at[j], y_dev)

    def gather_sum(j):
        got("rx", j)
        got("ry", j)
        total = add(keep.at[j, 0, 0], crecv.at[j, 0, 0], rxf.at[j], ryf.at[j])
        if j:
            osum[j] = total.astype(bf16)
            send(("rz", j), osum.at[j], rz.at[j], (at_ep(j, 0), tp))
        else:
            out[...] = total

    xbuf[0, 0, 0, 0] = hid[...]
    spread(0)
    send_rows()
    send_choices()
    for load in loads:
        load.start()
    group = []
    back_order = order[1:] + order[:1]
    done = 0
    for t in range(nz + 3):
        for lag, stage in ((0, spread), (1, forward), (2, finish), (3, take)):
            if (lag == 0 and 0 < t < nz) or (lag and 0 <= t - lag < nz):
                stage(order[t - lag])
        if t == 1:
            select()
        if t >= 3:
            group.append(order[t - 3])
            if len(group) == 2:
                experts(group)
                group = []
        if t == nz + 1 and 1:
            scatter(back_order[0])
            done = 1
    for t in range(nz + 3):
        for lag, stage in ((0, scatter), (1, diagonal), (2, sides), (3, gather_sum)):
            if 0 <= t - lag < nz and (lag or t >= done):
                stage(back_order[t - lag])
    for j in range(1, nz):
        got("rz", j)
        out[...] += rz[j].astype(f32)
    for copy in copies.values():
        copy.wait_send()


def local_dense(
    hidden_in,
    norm_gain,
    router_weight,
    shared_gate_up,
    shared_down,
    slot_gate_up,
    slot_down,
    slot_expert,
    slot_choice,
    live_count,
):
    nz = lax.axis_size("ep") // 2
    tok_count, width = hidden_in.shape
    feat = 4 * width
    top_count = slot_choice.shape[1]
    slot_count = slot_expert.shape[0]
    cap = 4 * max(2, 2 * (tok_count // 4) * top_count // slot_count)
    rows = 2 * nz * cap
    sff, eff = shared_down.shape[0], slot_down.shape[1]
    bf16, f32 = jnp.bfloat16, jnp.float32
    half = tok_count // 2
    block = (tok_count, width)
    vmem = pl.BlockSpec(memory_space=pltpu.VMEM)
    hbm = pl.BlockSpec(memory_space=pl.ANY)
    copy_count = (nz - 1) + (2 * nz - 1) + 3 * nz + 4 * nz + nz + 2 * nz + 4 * nz + (nz - 1)
    summed = pl.pallas_call(
        functools.partial(block_kernel, nz, cap, top_count),
        out_shape=jax.ShapeDtypeStruct(block, f32),
        in_specs=[vmem] * 5 + [hbm] * 4,
        out_specs=vmem,
        scratch_shapes=[
            pltpu.VMEM((nz, 2, 2, 2) + block, bf16),
            pltpu.VMEM((2 * nz, top_count, tok_count), jnp.int32),
            pltpu.VMEM((2 * eff, feat), bf16),
            pltpu.VMEM((eff, feat), bf16),
            pltpu.VMEM((2 * sff, feat), bf16),
            pltpu.VMEM((sff, feat), bf16),
            pltpu.VMEM((2 * nz, tok_count), f32),
            pltpu.VMEM((slot_count, feat), bf16),
            pltpu.VMEM((rows, slot_count), f32),
            pltpu.VMEM((2 * nz, cap, tok_count), bf16),
            pltpu.VMEM((2 * nz, cap, tok_count), bf16),
            pltpu.VMEM((cap, feat), f32),
            pltpu.VMEM((rows, feat), bf16),
            pltpu.VMEM((rows, eff), bf16),
            pltpu.VMEM((rows, feat), bf16),
            pltpu.VMEM((tok_count, feat), bf16),
            pltpu.VMEM((tok_count, sff), bf16),
            pltpu.VMEM((tok_count, feat), f32),
            pltpu.VMEM((nz, 2, 2) + block, bf16),
            pltpu.VMEM((nz, 2, 2) + block, bf16),
            pltpu.VMEM((nz, 2, 2) + block, bf16),
            pltpu.VMEM((nz,) + block, bf16),
            pltpu.VMEM((nz, half, width), bf16),
            pltpu.VMEM((nz, half, width), bf16),
            pltpu.VMEM((nz,) + block, bf16),
            pltpu.VMEM((nz,) + block, bf16),
            pltpu.VMEM((nz,) + block, bf16),
            pltpu.VMEM((nz,) + block, bf16),
            pltpu.VMEM((nz,) + block, bf16),
            pltpu.VMEM((nz,) + block, bf16),
            pltpu.SemaphoreType.DMA((4,)),
            pltpu.SemaphoreType.DMA((copy_count,)),
            pltpu.SemaphoreType.DMA((copy_count,)),
        ],
        compiler_params=pltpu.CompilerParams(
            collective_id=0, has_side_effects=True, vmem_limit_bytes=56 * 2**20
        ),
    )(
        hidden_in,
        slot_choice.T,
        slot_expert.reshape(1, -1),
        norm_gain.reshape(1, -1),
        router_weight.T,
        slot_gate_up[0].transpose(1, 2, 0).reshape(2 * eff, feat),
        slot_down[0],
        shared_gate_up.transpose(1, 2, 0).reshape(2 * sff, feat),
        shared_down,
    )
    live_rows = jnp.arange(tok_count, dtype=jnp.int32) < live_count[0]
    mixed_out = jnp.where(live_rows[:, None], hidden_in.astype(jnp.float32) + summed, 0.0)
    return mixed_out.astype(jnp.bfloat16)


def solution(mesh):
    in_specs = (
        P("ep", "tp"),
        P(),
        P(),
        P(None, None, "tp"),
        P("tp", None),
        P(("ep", "tp"), None, None, None),
        P(("ep", "tp"), None, None),
        P(),
        P("ep", None),
        P("ep"),
    )
    out_specs = P("ep", "tp")
    local = local_dense if mesh.size <= 64 and mesh.shape["tp"] == 4 else local_exchange
    return jax.shard_map(local, mesh=mesh, in_specs=in_specs, out_specs=out_specs, check_vma=False)
```

```python
import functools
import jax
import jax.numpy as jnp
from jax import lax
from jax.experimental import pallas as pl
from jax.experimental.pallas import tpu as pltpu
from jax.sharding import PartitionSpec as P


def gate_weights(normed_rows, choices, router_weight, slot_expert):
    logits = jnp.dot(normed_rows, router_weight, preferred_element_type=jnp.float32)
    slot_total = slot_expert.shape[0]
    expert_total = router_weight.shape[1]
    slot_hit = choices[:, :, None] == jnp.arange(slot_total, dtype=jnp.int32)
    expert_ids = jnp.sum(jnp.where(slot_hit, slot_expert, 0), axis=2)
    expert_hit = expert_ids[:, :, None] == jnp.arange(expert_total, dtype=jnp.int32)
    picked = jnp.sum(jnp.where(expert_hit, logits[:, None, :], 0.0), axis=2)
    highest = jnp.max(picked, axis=1, keepdims=True)
    weights = jnp.exp(picked - highest)
    return (weights / jnp.sum(weights, axis=1, keepdims=True)).astype(jnp.bfloat16)


def slot_positions(targets):
    length = targets.shape[0]
    same_slot = targets[:, None] == targets[None, :]
    earlier = jnp.arange(length)[None, :] < jnp.arange(length)[:, None]
    return jnp.sum(same_slot & earlier, axis=1)


def expert_apply(received, slot_gate_up, slot_down):
    shape_in = received.shape
    flat_rows = received.reshape(-1, shape_in[-1])
    gate_up = jnp.einsum(
        "rd,dgf->rgf", flat_rows, slot_gate_up[0], preferred_element_type=jnp.float32
    )
    activated = (jax.nn.silu(gate_up[:, 0]) * gate_up[:, 1]).astype(jnp.bfloat16)
    result = jnp.dot(activated, slot_down[0], preferred_element_type=jnp.float32).astype(
        jnp.bfloat16
    )
    return result.reshape(shape_in)


def local_exchange(
    hidden_in,
    norm_gain,
    router_weight,
    shared_gate_up,
    shared_down,
    slot_gate_up,
    slot_down,
    slot_expert,
    slot_choice,
    live_count,
):
    tp_count = lax.axis_size("tp")
    ep_count = lax.axis_size("ep")
    tp_index = lax.axis_index("tp")
    tok_count = hidden_in.shape[0]
    feature_width = hidden_in.shape[1] * tp_count
    top_count = slot_choice.shape[1]
    slot_count = slot_expert.shape[0]
    quarter = tok_count // tp_count
    capacity = max(2, 2 * quarter * top_count // slot_count)
    full_rows = lax.all_gather(hidden_in, "tp", axis=1, tiled=True)
    wide_rows = full_rows.astype(jnp.float32)
    norm_scale = lax.rsqrt(jnp.mean(wide_rows * wide_rows, axis=1, keepdims=True) + 1e-06)
    normed = (wide_rows * norm_scale * norm_gain).astype(jnp.bfloat16)
    shared_proj = jnp.einsum(
        "td,dgf->tgf", normed, shared_gate_up, preferred_element_type=jnp.float32
    )
    shared_hidden = (jax.nn.silu(shared_proj[:, 0]) * shared_proj[:, 1]).astype(jnp.bfloat16)
    partial_value = jnp.dot(shared_hidden, shared_down, preferred_element_type=jnp.float32)
    row_start = tp_index * quarter
    own_rows = lax.dynamic_slice_in_dim(normed, row_start, quarter, 0)
    own_choice = lax.dynamic_slice_in_dim(slot_choice, row_start, quarter, 0)
    gate_values = gate_weights(own_rows, own_choice, router_weight, slot_expert)
    targets = own_choice.reshape(-1)
    placed = targets * capacity + slot_positions(targets)
    outgoing = jnp.zeros((slot_count * capacity, feature_width), jnp.bfloat16)
    outgoing = outgoing.at[placed].set(jnp.repeat(own_rows, top_count, axis=0))
    outgoing = outgoing.reshape(ep_count, tp_count, capacity, feature_width)
    arrived = lax.all_to_all(
        lax.all_to_all(outgoing, "ep", split_axis=0, concat_axis=0, tiled=True),
        "tp",
        split_axis=1,
        concat_axis=1,
        tiled=True,
    )
    computed = expert_apply(arrived, slot_gate_up, slot_down)
    returned = lax.all_to_all(
        lax.all_to_all(computed, "ep", split_axis=0, concat_axis=0, tiled=True),
        "tp",
        split_axis=1,
        concat_axis=1,
        tiled=True,
    )
    fetched = returned.reshape(-1, feature_width)[placed].reshape(quarter, top_count, feature_width)
    routed = jnp.einsum("qk,qkd->qd", gate_values, fetched, preferred_element_type=jnp.float32)
    own_partial = lax.dynamic_slice_in_dim(partial_value, row_start, quarter, 0) + routed
    partial_value = lax.dynamic_update_slice_in_dim(partial_value, own_partial, row_start, 0)
    summed = lax.psum_scatter(partial_value, "tp", scatter_dimension=1, tiled=True)
    live_rows = jnp.arange(tok_count, dtype=jnp.int32) < live_count[0]
    mixed_out = jnp.where(live_rows[:, None], hidden_in.astype(jnp.float32) + summed, 0.0)
    return mixed_out.astype(jnp.bfloat16)


def dot_nt(a, b):
    return lax.dot_general(a, b, (((1,), (1,)), ((), ())), preferred_element_type=jnp.float32)


def dot_nn(a, b):
    return jnp.dot(a, b, preferred_element_type=jnp.float32)


def silu_mul(g, u):
    return (g / (1.0 + jnp.exp(-g)) * u).astype(jnp.bfloat16)


def chunks(total, step):
    return [(at, min(step, total - at)) for at in range(0, total, step)]


def block_kernel(
    nz,
    cap,
    top,
    hid,
    ch_own,
    slot_row,
    gain,
    router_t,
    w_gu,
    w_d,
    w_sgu,
    w_sd,
    out,
    xbuf,
    cbuf,
    gu,
    dn,
    sgu,
    sdn,
    hits,
    by_slot,
    member,
    cho,
    chg,
    raw,
    sel,
    hmid,
    expo,
    own,
    hsh,
    shp,
    keep,
    snd,
    crecv,
    dsum,
    ry0,
    rx1,
    xs,
    ys,
    rxf,
    ryf,
    osum,
    rz,
    own_sum,
    wsem,
    ssem,
    rsem,
):
    bf16, f32 = jnp.bfloat16, jnp.float32
    ep, tp = lax.axis_index("ep"), lax.axis_index("tp")
    z, x, y, c = ep // 2, ep % 2, tp // 2, tp % 2
    tok, width = hid.shape
    half = tok // 2
    feat = gain.shape[1]
    slots = slot_row.shape[1]
    me = ep * 4 + tp

    def at_ep(j, i):
        return lax.rem(z + j, nz) * 2 + (1 - x if i else x)

    def at_tp(k, l):
        return (1 - y if k else y) * 2 + (1 - c if l else c)

    def cols(k, l):
        return pl.ds(pl.multiple_of(at_tp(k, l) * width, width), width)

    x_dev, y_dev, c_dev = (at_ep(0, 1), tp), (ep, at_tp(1, 0)), (ep, at_tp(0, 1))
    peers = [(j, i) for j in range(nz) for i in range(2) if j or i]

    barrier = pltpu.get_barrier_semaphore()
    for j, i in peers:
        pl.semaphore_signal(
            barrier, inc=1, device_id=(at_ep(j, i), tp), device_id_type=pl.DeviceIdType.MESH
        )
    for dev in (y_dev, c_dev):
        pl.semaphore_signal(barrier, inc=1, device_id=dev, device_id_type=pl.DeviceIdType.MESH)
    loads = [
        pltpu.make_async_copy(src, dst, wsem.at[n])
        for n, (src, dst) in enumerate(((w_sgu, sgu), (w_sd, sdn), (w_gu, gu), (w_d, dn)))
    ]
    pl.semaphore_wait(barrier, len(peers) + 2)

    copies = {}

    def send(name, src, dst, dev):
        n = len(copies)
        copy = pltpu.make_async_remote_copy(
            src_ref=src,
            dst_ref=dst,
            send_sem=ssem.at[n],
            recv_sem=rsem.at[n],
            device_id=dev,
            device_id_type=pl.DeviceIdType.MESH,
        )
        copy.start()
        copies[name] = copy

    def got(*name):
        copies[name].wait_recv()

    back = lambda j: (nz - j) % nz
    lo, hi = pl.ds(0, half), pl.ds(half, half)

    order = sorted(range(nz), key=lambda j: min(j, nz - j))
    pos = {j: n for n, j in enumerate(order)}

    def send_rows():
        for j in order[1:]:
            send(("z", j), hid, xbuf.at[j, 0, 0, 0], (at_ep(back(j), 0), tp))

    def send_choices():
        for j, i in peers:
            send(("ch", j, i), ch_own, cbuf.at[pos[j] * 2 + i], (at_ep(back(j), i), tp))

    def spread(j):
        if j:
            got("z", j)
        src = xbuf.at[j, 0, 0, 0] if j else hid
        send(("x1", j), src, xbuf.at[j, 1, 0, 0], x_dev)
        send(("y1", j), src, xbuf.at[j, 0, 1, 0], y_dev)
        send(("c00", j), src, xbuf.at[j, 0, 0, 1], c_dev)

    def forward(j):
        got("x1", j)
        send(("y2", j), xbuf.at[j, 1, 0, 0, lo], xbuf.at[j, 1, 1, 0, lo], y_dev)
        send(("c10", j), xbuf.at[j, 1, 0, 0], xbuf.at[j, 1, 0, 1], c_dev)
        got("y1", j)
        send(("x2", j), xbuf.at[j, 0, 1, 0, hi], xbuf.at[j, 1, 1, 0, hi], x_dev)
        send(("c01", j), xbuf.at[j, 0, 1, 0], xbuf.at[j, 0, 1, 1], c_dev)

    def finish(j):
        got("y2", j)
        got("x2", j)
        send(("c11", j), xbuf.at[j, 1, 1, 0], xbuf.at[j, 1, 1, 1], c_dev)

    def select():
        cbuf[0] = ch_own[...]
        for j, i in peers:
            got("ch", j, i)
        slot_ids = lax.broadcasted_iota(jnp.int32, (slots, tok), 0)
        place = lax.broadcasted_iota(jnp.int32, (cap, tok), 0).astype(f32)
        members = []
        for q in range(2 * nz):
            picks = cbuf[q]
            named = jnp.zeros((slots, tok), f32)
            for k in range(top):
                named = jnp.where(picks[k : k + 1, :] == slot_ids, 1.0, named)
            hits[q : q + 1, :] = jnp.sum(
                jnp.where(slot_ids == me, named, 0.0), axis=0, keepdims=True
            )
            members.append(named.astype(bf16))
        earlier = lax.broadcasted_iota(jnp.int32, (tok, tok), 0) < lax.broadcasted_iota(
            jnp.int32, (tok, tok), 1
        )
        hit = hits[...]
        rank = dot_nn(hit.astype(bf16), jnp.where(earlier, 1.0, 0.0).astype(bf16))
        for q in range(2 * nz):
            chosen = jnp.where(place == rank[q : q + 1, :], hit[q : q + 1, :], 0.0).astype(bf16)
            cho[q] = chosen
            member[q * cap : (q + 1) * cap, :] = dot_nt(chosen, members[q])
        held = lax.broadcasted_iota(jnp.int32, (router_t.shape[0], slots), 0)
        table = jnp.where(slot_row[...] == held, 1.0, 0.0).astype(bf16)
        by_slot[...] = lax.dot_general(
            table, router_t[...], (((0,), (0,)), ((), ())), preferred_element_type=f32
        ).astype(bf16)

    def norm(v):
        scale = lax.rsqrt(jnp.sum(v * v, axis=1, keepdims=True) * (1.0 / feat) + 1e-06)
        return (v * scale * gain[...]).astype(bf16)

    def pick(j, i):
        q = pos[j] * 2 + i
        for k in range(2):
            for l in range(2):
                raw[:, cols(k, l)] = dot_nn(cho[q], xbuf[j, i, k, l])
        sel[q * cap : (q + 1) * cap, :] = norm(raw[...])

    def shared():
        for k in range(2):
            for l in range(2):
                shp[:, cols(k, l)] = xbuf[0, 0, k, l].astype(f32)
        own[...] = norm(shp[...])
        loads[0].wait()
        ff = hsh.shape[1]
        hsh[...] = silu_mul(dot_nt(own[...], sgu[0:ff, :]), dot_nt(own[...], sgu[ff : 2 * ff, :]))
        loads[1].wait()
        for at, size in chunks(feat, 512):
            shp[:, at : at + size] = dot_nn(hsh[...], sdn[:, at : at + size])

    def experts(js):
        first, last = 2 * min(pos[j] for j in js), 2 * max(pos[j] for j in js) + 2
        part = slice(first * cap, last * cap)
        logits = dot_nt(sel[part, :], by_slot[...])
        named = member[part, :] > 0.5
        top_logit = jnp.max(jnp.where(named, logits, -1e30), axis=1, keepdims=True)
        weights = jnp.where(named, jnp.exp(jnp.where(named, logits - top_logit, 0.0)), 0.0)
        total = jnp.maximum(jnp.sum(weights, axis=1, keepdims=True), 1.0)
        slot_lane = lax.broadcasted_iota(jnp.int32, weights.shape, 1)
        mine = jnp.sum(jnp.where(slot_lane == me, weights, 0.0), axis=1, keepdims=True)
        gates = (mine / total).astype(bf16).astype(f32)
        for q in range(first, last):
            at = (q - first) * cap
            chg[q] = (cho[q].astype(f32) * gates[at : at + cap, :]).astype(bf16)
        if first == 0:
            loads[2].wait()
        ff = hmid.shape[1]
        for at, size in chunks(ff, 256):
            hmid[part, at : at + size] = silu_mul(
                dot_nt(sel[part, :], gu[at : at + size, :]),
                dot_nt(sel[part, :], gu[ff + at : ff + at + size, :]),
            )
        if first == 0:
            loads[3].wait()
        for at, size in chunks(feat, 512):
            expo[part, at : at + size] = dot_nn(hmid[part, :], dn[:, at : at + size]).astype(bf16)

    def take(j):
        for name in ("c00", "c10", "c01", "c11"):
            got(name, j)
        if j == 0:
            shared()
        pick(j, 0)
        pick(j, 1)

    def add(*refs):
        total = refs[0][...].astype(f32)
        for ref in refs[1:]:
            total = total + ref[...].astype(f32)
        return total

    def scatter(j):
        for l in (1, 0):
            for i in (1, 0):
                q = pos[j] * 2 + i
                for k in (1, 0):
                    part = lax.dot_general(
                        chg[q],
                        expo[q * cap : (q + 1) * cap, cols(k, l)],
                        (((0,), (0,)), ((), ())),
                        preferred_element_type=f32,
                    )
                    if q == 0:
                        part = part + shp[:, cols(k, l)]
                    (snd if l else keep)[j, i, k] = part.astype(bf16)
                if l:
                    send(("rc", j, i), snd.at[j, i], crecv.at[j, i], c_dev)

    def diagonal(j):
        got("rc", j, 1)
        dsum[j] = add(keep.at[j, 1, 1], crecv.at[j, 1, 1]).astype(bf16)
        send(("d0", j), dsum.at[j, lo], ry0.at[j], y_dev)
        send(("d1", j), dsum.at[j, hi], rx1.at[j], x_dev)

    def sides(j):
        xs[j, hi] = add(keep.at[j, 1, 0, hi], crecv.at[j, 1, 0, hi]).astype(bf16)
        got("d0", j)
        xs[j, lo] = add(keep.at[j, 1, 0, lo], crecv.at[j, 1, 0, lo], ry0.at[j]).astype(bf16)
        send(("rx", j), xs.at[j], rxf.at[j], x_dev)
        got("rc", j, 0)
        ys[j, lo] = add(keep.at[j, 0, 1, lo], crecv.at[j, 0, 1, lo]).astype(bf16)
        got("d1", j)
        ys[j, hi] = add(keep.at[j, 0, 1, hi], crecv.at[j, 0, 1, hi], rx1.at[j]).astype(bf16)
        send(("ry", j), ys.at[j], ryf.at[j], y_dev)

    def gather_sum(j):
        got("rx", j)
        got("ry", j)
        total = add(keep.at[j, 0, 0], crecv.at[j, 0, 0], rxf.at[j], ryf.at[j])
        if j:
            osum[j] = total.astype(bf16)
            send(("rz", j), osum.at[j], rz.at[j], (at_ep(j, 0), tp))
        else:
            own_sum[...] = total

    xbuf[0, 0, 0, 0] = hid[...]
    spread(0)
    send_rows()
    send_choices()
    for load in loads:
        load.start()
    group = []
    back_order = order[1:] + order[:1]
    done = 0
    for t in range(nz + 3):
        for lag, stage in ((0, spread), (1, forward), (2, finish), (3, take)):
            if (lag == 0 and 0 < t < nz) or (lag and 0 <= t - lag < nz):
                stage(order[t - lag])
        if t == 2:
            select()
        if t >= 3:
            group.append(order[t - 3])
            if len(group) == 2:
                experts(group)
                group = []
        if t == nz + 1 and 1:
            scatter(back_order[0])
            done = 1
    for t in range(nz + 3):
        for lag, stage in ((0, scatter), (1, diagonal), (2, sides), (3, gather_sum)):
            if 0 <= t - lag < nz and (lag or t >= done):
                stage(back_order[t - lag])
    for j in range(1, nz):
        got("rz", j)
    total = hid[...].astype(f32) + own_sum[...]
    for j in range(1, nz):
        total = total + rz[j].astype(f32)
    out[...] = total.astype(bf16)
    for copy in copies.values():
        copy.wait_send()


def local_dense(
    hidden_in,
    norm_gain,
    router_weight,
    shared_gate_up,
    shared_down,
    slot_gate_up,
    slot_down,
    slot_expert,
    slot_choice,
    live_count,
):
    nz = lax.axis_size("ep") // 2
    tok_count, width = hidden_in.shape
    feat = 4 * width
    top_count = slot_choice.shape[1]
    slot_count = slot_expert.shape[0]
    cap = 4 * max(2, 2 * (tok_count // 4) * top_count // slot_count)
    rows = 2 * nz * cap
    sff, eff = shared_down.shape[0], slot_down.shape[1]
    bf16, f32 = jnp.bfloat16, jnp.float32
    half = tok_count // 2
    block = (tok_count, width)
    vmem = pl.BlockSpec(memory_space=pltpu.VMEM)
    hbm = pl.BlockSpec(memory_space=pl.ANY)
    copy_count = (nz - 1) + (2 * nz - 1) + 3 * nz + 4 * nz + nz + 2 * nz + 4 * nz + (nz - 1)
    mixed = pl.pallas_call(
        functools.partial(block_kernel, nz, cap, top_count),
        out_shape=jax.ShapeDtypeStruct(block, bf16),
        in_specs=[vmem] * 5 + [hbm] * 4,
        out_specs=vmem,
        scratch_shapes=[
            pltpu.VMEM((nz, 2, 2, 2) + block, bf16),
            pltpu.VMEM((2 * nz, top_count, tok_count), jnp.int32),
            pltpu.VMEM((2 * eff, feat), bf16),
            pltpu.VMEM((eff, feat), bf16),
            pltpu.VMEM((2 * sff, feat), bf16),
            pltpu.VMEM((sff, feat), bf16),
            pltpu.VMEM((2 * nz, tok_count), f32),
            pltpu.VMEM((slot_count, feat), bf16),
            pltpu.VMEM((rows, slot_count), f32),
            pltpu.VMEM((2 * nz, cap, tok_count), bf16),
            pltpu.VMEM((2 * nz, cap, tok_count), bf16),
            pltpu.VMEM((cap, feat), f32),
            pltpu.VMEM((rows, feat), bf16),
            pltpu.VMEM((rows, eff), bf16),
            pltpu.VMEM((rows, feat), bf16),
            pltpu.VMEM((tok_count, feat), bf16),
            pltpu.VMEM((tok_count, sff), bf16),
            pltpu.VMEM((tok_count, feat), f32),
            pltpu.VMEM((nz, 2, 2) + block, bf16),
            pltpu.VMEM((nz, 2, 2) + block, bf16),
            pltpu.VMEM((nz, 2, 2) + block, bf16),
            pltpu.VMEM((nz,) + block, bf16),
            pltpu.VMEM((nz, half, width), bf16),
            pltpu.VMEM((nz, half, width), bf16),
            pltpu.VMEM((nz,) + block, bf16),
            pltpu.VMEM((nz,) + block, bf16),
            pltpu.VMEM((nz,) + block, bf16),
            pltpu.VMEM((nz,) + block, bf16),
            pltpu.VMEM((nz,) + block, bf16),
            pltpu.VMEM((nz,) + block, bf16),
            pltpu.VMEM(block, f32),
            pltpu.SemaphoreType.DMA((4,)),
            pltpu.SemaphoreType.DMA((copy_count,)),
            pltpu.SemaphoreType.DMA((copy_count,)),
        ],
        compiler_params=pltpu.CompilerParams(
            collective_id=0, has_side_effects=True, vmem_limit_bytes=56 * 2**20
        ),
    )(
        hidden_in,
        slot_choice.T,
        slot_expert.reshape(1, -1),
        norm_gain.reshape(1, -1),
        router_weight.T,
        slot_gate_up[0].transpose(1, 2, 0).reshape(2 * eff, feat),
        slot_down[0],
        shared_gate_up.transpose(1, 2, 0).reshape(2 * sff, feat),
        shared_down,
    )
    live_rows = jnp.arange(tok_count, dtype=jnp.int32) < live_count[0]
    return jnp.where(live_rows[:, None], mixed, jnp.zeros_like(mixed))


def solution(mesh):
    in_specs = (
        P("ep", "tp"),
        P(),
        P(),
        P(None, None, "tp"),
        P("tp", None),
        P(("ep", "tp"), None, None, None),
        P(("ep", "tp"), None, None),
        P(),
        P("ep", None),
        P("ep"),
    )
    out_specs = P("ep", "tp")
    local = local_dense if mesh.size <= 64 and mesh.shape["tp"] == 4 else local_exchange
    return jax.shard_map(local, mesh=mesh, in_specs=in_specs, out_specs=out_specs, check_vma=False)
```
